256 devices in a mesh: dom: 8 (over z), lat: 32 (over y, x, core).
Axes of the slice: x: 4, y: 4, z: 8, core: 2. Of those that a mesh axis runs over, the one named last changes fastest.
Arguments:
- ensemble: float32 [16, 3, 256, 4096], P('dom', None, 'lat'), may hold values from -6 to 6
- perturbation: float32 [16, 3, 256, 4096], P('dom', None, 'lat'), may hold values from -4 to 4
- parents: int32 [16], replicated, may hold values from 0 to 15, as said below
- depth: float32 [256, 4096], P('lat'), may hold values from 0.5 to 2
Outputs:
- forecast: float32 [16, 3, 256, 4096], P('dom', None, 'lat')
The draws below stay inside these ranges and needn't reach their ends.
Inputs may be any that keep to these rules, and one draw needn't show every extreme that they name: parents[j] is the member whose fields the new member j copies; every aligned block of 2 members holds a member that some entry names.
All inputs are finite; a program needn't handle non-finite values.
Results may differ from the reference program's by a relative error of at most 0.00014.
Values sent between devices are 32-bit elements; how exact they have to be, the bound alone decides.
No kernel may reach another device: no remote copies, remote signals or barrier semaphores. Data moves between devices by JAX's collectives and lax.ppermute only.
A program may use at most 128 MiB of HBM per device.

```python
import math
import jax
import jax.numpy as jnp
from jax import lax

MEMBERS_PER_SHARD = 2
PARTICLES = 16
NLAT = 256
NLON = 4096
STEPS = 4


def draw_parents(key, part):
    slot_key, rest_key = jax.random.split(jax.random.fold_in(key, 7))
    member_groups = PARTICLES // MEMBERS_PER_SHARD
    groups = jnp.arange(member_groups, dtype=jnp.int32)
    far_groups = (groups + member_groups // 2) % member_groups
    far_parents = far_groups * MEMBERS_PER_SHARD + jax.random.randint(slot_key, (member_groups,), 0, MEMBERS_PER_SHARD, dtype=jnp.int32)
    other_parents = jax.random.randint(rest_key, (member_groups, MEMBERS_PER_SHARD - 1), 0, PARTICLES, dtype=jnp.int32)
    table = jnp.concatenate([far_parents[:, None], other_parents], axis=1)
    return table.reshape((PARTICLES,)).astype(jnp.int32)


def block_levels(stream_key, extent, cuts, smallest, top_value):
    loudness, own = 1.0, jax.random.fold_in(stream_key, 6)
    for position, parts in cuts:
        draws = jnp.exp(jax.random.uniform(jax.random.fold_in(own, position), (parts,), jnp.float32, smallest / len(cuts), top_value / len(cuts)))
        loudness = loudness * jnp.repeat(draws, extent[position] // parts).reshape([-1 if axis == position else 1 for axis in range(len(extent))])
    return loudness


def centred(rng, shape, deviation, limit, shards=(), held_as=jnp.bfloat16):
    gain = block_levels(rng, shape, shards, -0.22, 0.18) if shards else 1.0
    values = jax.random.normal(rng, shape, jnp.float32) * deviation * gain
    return jnp.minimum(jnp.maximum(values, -limit), limit).astype(held_as)


def setup_inputs(seed: int = 0) -> dict:
    keys = jax.random.split(jax.random.key(seed), 5)
    ensemble = centred(keys[0], (PARTICLES, 3, NLAT, NLON), 1.0, 6.0, ((0, 8), (2, 32)), jnp.float32)
    perturbation = centred(keys[1], (PARTICLES, 3, NLAT, NLON), 0.3, 4.0, ((0, 8), (2, 32)), jnp.float32)
    parents = draw_parents(jax.random.fold_in(keys[4], 71), 0)
    depth = jnp.clip(jnp.exp(math.log(2.0) - 1.3862944 * jax.random.uniform(keys[3], (NLAT, NLON), jnp.float32) ** block_levels(keys[3], (NLAT, NLON), ((0, 32),), -0.2, 0.2)), 0.5, 2.0)
    return {"ensemble": ensemble, "perturbation": perturbation, "parents": parents, "depth": depth}


time_step = 0.8


def tendency(padded, depth_pad, coriolis):
    surface_height = padded[..., 0, :, :]
    east = padded[..., 1, :, :]
    north = padded[..., 2, :, :]
    flux_east = depth_pad * east
    flux_north = depth_pad * north

    def across(field):
        return (0.5 * (jnp.roll(field, -1, -1) - jnp.roll(field, 1, -1)))[..., 1:-1, :]

    def along(field):
        return 0.5 * (field[..., 2:, :] - field[..., :-2, :])

    rate_h = -(across(flux_east) + along(flux_north))
    rate_u = -across(surface_height) + coriolis * north[..., 1:-1, :]
    rate_v = -along(surface_height) - coriolis * east[..., 1:-1, :]
    return jnp.stack([rate_h, rate_u, rate_v], axis=-3)


def reference(ensemble, perturbation, parents, depth):
    copied = jnp.take(ensemble, parents.astype(jnp.int32), axis=0) + perturbation
    coriolis = (0.4 * ((2.0 * jnp.arange(NLAT, dtype=jnp.float32) + 1.0) / NLAT - 1.0))[:, None]
    depth_pad = jnp.pad(depth, ((1, 1), (0, 0)))

    def rate(state):
        return tendency(jnp.pad(state, ((0, 0), (1, 1), (0, 0))), depth_pad, coriolis)

    def member(state):
        for step in range(STEPS):
            first = rate(state)
            later_value = rate(state + (0.5 * time_step) * first)
            third = rate(state + (0.5 * time_step) * later_value)
            fourth = rate(state + time_step * third)
            state = state + (time_step / 6.0) * (first + 2.0 * later_value + 2.0 * third + fourth)
        return state

    return lax.map(member, copied)
```

```python
import jax
import jax.numpy as jnp
from jax import lax
from jax.experimental import pallas as pl
from jax.experimental.pallas import tpu as pltpu
from jax.sharding import PartitionSpec as P

STEPS = 4
STEPS_PER_EXCHANGE = 2
TIME_STEP = 0.8
LANES = 128
SUBLANES = 8
REACH = 4 * STEPS_PER_EXCHANGE
ROUNDS = 4
CHAINS = 2
UNROLL = 32
VMEM_LIMIT = 16 * 2**20


def to_tiles(strip):
    *lead, rows, lon = strip.shape
    split = strip.reshape(*lead, rows, lon // LANES, LANES)
    return jnp.swapaxes(split, -3, -2).reshape(*lead, lon // LANES * rows, LANES)


def from_tiles(tiles, rows):
    *lead, count, _ = tiles.shape
    split = tiles.reshape(*lead, count // rows, rows, LANES)
    return jnp.swapaxes(split, -3, -2).reshape(*lead, rows, count // rows * LANES)


def neighbour(value, axis, shift, wrap=False):
    devices = lax.axis_size(axis)
    pairs = [(i, (i + shift) % devices) for i in range(devices) if wrap or 0 <= i + shift < devices]
    return lax.ppermute(value, axis, pairs)


def both_sides(value):
    return neighbour(value, "lat", 1), neighbour(value, "lat", -1)


def where_row(row, chunk, rows, chunks):
    return pl.ds(chunk * rows + row, SUBLANES, stride=chunks * rows)


def choose(table_ref, row, identities, candidates):
    wanted = table_ref[row]
    value = candidates[0]
    for identity, candidate in zip(identities[1:], candidates[1:]):
        value = jnp.where(wanted == table_ref[identity], candidate, value)
    return value


def plan_kernel(devices, per, rounds, me_ref, parents_ref, table_ref, case_ref):
    count = devices * per
    pairs = 2 * count
    half = devices // 2
    me = me_ref[0]
    down_row = lax.broadcasted_iota(jnp.int32, (pairs, LANES), 0)
    along_row = lax.broadcasted_iota(jnp.int32, (pairs, LANES), 1)

    def facts(index):
        item = lax.rem(index, count)
        return index // count, item, item // per

    sides = [facts(index) for index in (down_row, along_row)]
    far = [jnp.zeros((pairs, LANES), jnp.int32) for _ in range(2)]
    for entry in range(count):
        parent = parents_ref[entry]
        origin = parent // per
        hops = lax.rem(entry // per - origin + devices, devices)
        goes_up = jnp.logical_or(hops < half, jnp.logical_and(hops == half, lax.rem(origin, 2) == 0))
        slot = parent + jnp.where(goes_up, 0, count)
        distance = jnp.where(goes_up, hops, devices - hops)
        far = [jnp.maximum(f, jnp.where(index == slot, distance, 0)) for f, index in zip(far, (down_row, along_row))]

    def put(row, value):
        table_ref[row] = jnp.broadcast_to(value, (SUBLANES, LANES)).astype(jnp.int32)

    for k in range(per):
        put(k, jnp.full((SUBLANES, LANES), me * per + k, jnp.int32))
        put(per + k, jnp.full((SUBLANES, LANES), parents_ref[me * per + k], jnp.int32))
    position = [jnp.zeros((pairs, LANES), jnp.int32) for _ in range(2)]
    unmet = []
    for r in range(rounds):
        left, link, key = [], [], []
        for (direction, item, origin), f, p, index in zip(sides, far, position, (down_row, along_row)):
            step = jnp.where(direction == 0, p, devices - p)
            left.append(f - p)
            link.append(lax.rem(origin + step, devices) + direction * devices)
            key.append(jnp.where(f > p, (f - p) * pairs + pairs - 1 - index, -1))
        same = link[0] == link[1]
        beaten_down = jnp.max(jnp.where(same & (key[1] > key[0]), 1, 0), axis=1, keepdims=True)
        beaten_along = jnp.max(jnp.where(same & (key[0] > key[1]), 1, 0), axis=0, keepdims=True)
        wins = [
            jnp.where((left[0] > 0) & (jnp.broadcast_to(beaten_down, left[0].shape) == 0), 1, 0),
            jnp.where((left[1] > 0) & (jnp.broadcast_to(beaten_along, left[1].shape) == 0), 1, 0),
        ]
        for q, (place, direction) in enumerate(((me, 0), (me + devices - 1, 0), (me, 1), (me + 1, 1))):
            here = (wins[1] > 0) & (link[1] == lax.rem(place, devices) + direction * devices)
            put(2 * per + 4 * r + q, jnp.max(jnp.where(here, sides[1][1], -1)[:SUBLANES], axis=1, keepdims=True))
        position = [p + w for p, w in zip(position, wins)]
        unmet.append(jnp.max(jnp.where(far[1] > position[1], 1, 0)[:SUBLANES], axis=1, keepdims=True))
    case_ref[...] = jnp.broadcast_to(unmet[-2] + unmet[-1], (SUBLANES, LANES))


def plan(parents, me, devices, per, rounds):
    smem = pl.BlockSpec(memory_space=pltpu.SMEM)
    vmem = pl.BlockSpec(memory_space=pltpu.VMEM)
    return pl.pallas_call(
        lambda *refs: plan_kernel(devices, per, rounds, *refs),
        out_shape=(
            jax.ShapeDtypeStruct((2 * per + 4 * rounds, SUBLANES, LANES), jnp.int32),
            jax.ShapeDtypeStruct((SUBLANES, LANES), jnp.int32),
        ),
        in_specs=[smem, smem],
        out_specs=(vmem, vmem),
        compiler_params=pltpu.CompilerParams(vmem_limit_bytes=VMEM_LIMIT),
        name="plan",
    )(me, parents)


def candidates_of(per, own_ref, received, field, base, rows):
    values = [own_ref[k, field, pl.ds(base, rows), :].reshape(-1, SUBLANES, LANES) for k in range(per)]
    return values + [ref[field].reshape(-1, SUBLANES, LANES) for ref in received]


def select_kernel(per, base, round_index, table_ref, own_ref, *refs):
    received, (up_ref, down_ref) = refs[:-2], refs[-2:]
    fields, rows, _ = up_ref.shape
    names = identity_rows(per, len(received))
    for f in range(fields):
        values = candidates_of(per, own_ref, received, f, base, rows)
        for out_ref, q in ((up_ref, 0), (down_ref, 2)):
            out_ref[f] = choose(table_ref, 2 * per + 4 * round_index + q, names, values).reshape(rows, LANES)


def identity_rows(per, received):
    return list(range(per)) + [2 * per + 4 * (k // 2) + (1, 3)[k % 2] for k in range(received)]


def select(table, own, received, base, rows, round_index):
    per, fields = own.shape[:2]
    vmem = pl.BlockSpec(memory_space=pltpu.VMEM)
    shape = jax.ShapeDtypeStruct((fields, rows, LANES), jnp.float32)
    return pl.pallas_call(
        lambda *refs: select_kernel(per, base, round_index, *refs),
        out_shape=(shape, shape),
        in_specs=[vmem] * (2 + len(received)),
        out_specs=(vmem, vmem),
        cost_estimate=pl.CostEstimate(flops=0, bytes_accessed=4 * fields * rows * LANES * 4, transcendentals=0),
        compiler_params=pltpu.CompilerParams(vmem_limit_bytes=VMEM_LIMIT),
        name="select",
    )(table, own, *received)


def spread(rows, value_ref, out_ref):
    fields = out_ref.shape[0]
    chunks = out_ref.shape[-1] // LANES

    def one_row(r, carry):
        for f in range(fields):
            for c in range(chunks):
                out_ref[f, r, :, pl.ds(c * LANES, LANES)] = value_ref[f, where_row(r, c, rows, chunks), :]
        return carry

    lax.fori_loop(0, rows, one_row, 0)


def collect_kernel(per, rows, entry, chains, table_ref, own_ref, noise_ref, *refs):
    out_ref, value_ref = refs[-2:]
    received = refs[:-2]
    each = len(received) // chains
    fields, count, _ = value_ref.shape
    part = count // chains
    names = identity_rows(per, each)
    for f in range(fields):
        for h in range(chains):
            values = candidates_of(per, own_ref, received[h * each:(h + 1) * each], f, h * part, part)
            found = choose(table_ref, per + entry, names, values).reshape(part, LANES)
            where = pl.ds(h * part, part)
            value_ref[f, where, :] = found + noise_ref[entry, f, where, :]
    spread(rows, value_ref, out_ref)


def collect(table, own, noise, chains, rows, entry):
    per, fields, count, _ = own.shape
    lon = count // rows * LANES
    vmem = pl.BlockSpec(memory_space=pltpu.VMEM)
    pieces = [piece for chain in chains for piece in chain]
    return pl.pallas_call(
        lambda *refs: collect_kernel(per, rows, entry, len(chains), *refs),
        out_shape=jax.ShapeDtypeStruct((fields, rows, SUBLANES, lon // SUBLANES), jnp.float32),
        in_specs=[vmem] * (3 + len(pieces)),
        out_specs=vmem,
        scratch_shapes=[pltpu.VMEM((fields, count, LANES), jnp.float32)],
        cost_estimate=pl.CostEstimate(flops=fields * rows * lon, bytes_accessed=12 * fields * rows * lon, transcendentals=0),
        compiler_params=pltpu.CompilerParams(vmem_limit_bytes=VMEM_LIMIT),
        name="collect",
    )(table, own, noise, *pieces)


def unpack_rows(rows, source):
    fields, count, _ = source.shape
    lon = count // rows * LANES
    vmem = pl.BlockSpec(memory_space=pltpu.VMEM)
    return pl.pallas_call(
        lambda *refs: spread(rows, *refs),
        out_shape=jax.ShapeDtypeStruct((fields, rows, SUBLANES, lon // SUBLANES), jnp.float32),
        in_specs=[vmem],
        out_specs=vmem,
        cost_estimate=pl.CostEstimate(flops=0, bytes_accessed=8 * fields * rows * lon, transcendentals=0),
        compiler_params=pltpu.CompilerParams(vmem_limit_bytes=VMEM_LIMIT),
        name="unpack",
    )(source)


def advance_kernel(rows, total_rows, final, place_ref, before, own, after, d_before, d_own, d_after, out_ref, state, first, second, third, depth):
    chunks = state.shape[-1] // LANES
    base_row = place_ref[0] * rows - REACH
    lane = lax.broadcasted_iota(jnp.int32, (SUBLANES, LANES), 1)
    at_start, at_end = lane == 0, lane == LANES - 1

    def lanes(c):
        return pl.ds(c * LANES, LANES)

    def load_row(ref, *index):
        return [ref[(*index, slice(None), lanes(c))] for c in range(chunks)]

    def difference_east(row):
        right = [pltpu.roll(v, 1, 1) for v in row]
        left = [pltpu.roll(v, LANES - 1, 1) for v in row]
        before_ = [pltpu.roll(right[-1], 1, 0)] + right[:-1]
        after_ = left[1:] + [pltpu.roll(left[0], SUBLANES - 1, 0)]
        return [
            jnp.where(at_start, b, r) - jnp.where(at_end, a, l)
            for b, r, a, l in zip(before_, right, after_, left)
        ]

    for block, (strip, d) in enumerate(((before, d_before), (own, d_own), (after, d_after))):
        state[:, block * rows:(block + 1) * rows] = strip[...]
        depth[block * rows:(block + 1) * rows] = d[...]

    def stage(source, low, high, emit):
        def flux(r):
            return [d * v for d, v in zip(load_row(depth, r), load_row(source, 2, r))]

        def one(r, carry):
            h_before, h_here, f_before, f_here = carry
            h_after, f_after = load_row(source, 0, r + 1), flux(r + 1)
            east, north = load_row(source, 1, r), load_row(source, 2, r)
            row = base_row + r
            turn = 0.8 * ((2 * row + 1).astype(jnp.float32) * (1.0 / total_rows) - 1.0)
            inside = jnp.logical_and(row >= 0, row < total_rows)
            dx_flux = difference_east([a * b for a, b in zip(load_row(depth, r), east)])
            dx_h = difference_east(h_here)
            rate_h = [x + (a - b) for x, a, b in zip(dx_flux, f_before, f_after)]
            rate_u = [x + turn * v for x, v in zip(dx_h, north)]
            rate_v = [(a - b) - turn * u for a, b, u in zip(h_before, h_after, east)]
            emit(r, inside, (rate_h, rate_u, rate_v))
            return h_here, h_after, f_here, f_after

        def several(count):
            def run(r, carry):
                for k in range(count):
                    carry = one(r + k, carry)
                return carry
            return run

        carry = (load_row(source, 0, low - 1), load_row(source, 0, low), flux(low - 1), flux(low))
        trips, rest = divmod(high - low, UNROLL)
        carry = lax.fori_loop(0, trips, lambda i, c: several(UNROLL)(low + UNROLL * i, c), carry)
        several(rest)(high - rest, carry)

    def advance(target, weight):
        def emit(r, inside, rates):
            scale = jnp.where(inside, jnp.float32(weight), jnp.float32(0.0))
            for f, rate in enumerate(rates):
                for c in range(chunks):
                    target[f, r, :, lanes(c)] = state[f, r, :, lanes(c)] + scale * rate[c]
        return emit

    def finish(last):
        def emit(r, inside, rates):
            scale = jnp.where(inside, jnp.float32(TIME_STEP / 12.0), jnp.float32(0.0))
            third_part = jnp.float32(1.0 / 3.0)
            for f, rate in enumerate(rates):
                for c in range(chunks):
                    y, a, b, d = (ref[f, r, :, lanes(c)] for ref in (state, first, second, third))
                    value = ((a - y) + (b + b + d)) * third_part + scale * rate[c]
                    if not last:
                        state[f, r, :, lanes(c)] = value
                    elif final:
                        out_ref[f, where_row(r - REACH, c, rows, chunks), :] = value
                    else:
                        out_ref[f, r - REACH, :, lanes(c)] = value
        return emit

    low, high = 0, 2 * REACH + rows
    for step in range(STEPS_PER_EXCHANGE):
        stage(state, low + 1, high - 1, advance(first, 0.25 * TIME_STEP))
        stage(first, low + 2, high - 2, advance(second, 0.25 * TIME_STEP))
        stage(second, low + 3, high - 3, advance(third, 0.5 * TIME_STEP))
        stage(third, low + 4, high - 4, finish(step == STEPS_PER_EXCHANGE - 1))
        low, high = low + 4, high - 4


def advance(strips, depth_strips, place, total_rows, final=None):
    fields, rows, _, width = strips[0].shape
    reach_rows = 2 * REACH + rows
    plane = pltpu.VMEM((fields, reach_rows, SUBLANES, width), jnp.float32)
    vmem = pl.BlockSpec(memory_space=pltpu.VMEM)
    smem = pl.BlockSpec(memory_space=pltpu.SMEM)
    operands = [place, *strips, *depth_strips]
    in_specs = [smem] + [vmem] * 6
    options = {}
    if final is None:
        out_shape, out_specs = strips[0].shape, vmem
    else:
        member, members, partial = final
        count = rows * SUBLANES * width // LANES
        out_shape = (members, fields, count, LANES)
        out_specs = pl.BlockSpec((None, fields, count, LANES), lambda i: (member, 0, 0, 0))
        if partial is not None:
            operands.append(partial)
            in_specs.append(pl.BlockSpec(memory_space=pl.ANY))
            options["input_output_aliases"] = {7: 0}

    def kernel(*refs):
        advance_kernel(rows, total_rows, final is not None, *refs[:7], *refs[-6:])

    return pl.pallas_call(
        kernel,
        grid=(1,),
        out_shape=jax.ShapeDtypeStruct(out_shape, jnp.float32),
        in_specs=in_specs,
        out_specs=out_specs,
        scratch_shapes=[plane] * 4 + [pltpu.VMEM((reach_rows, SUBLANES, width), jnp.float32)],
        compiler_params=pltpu.CompilerParams(vmem_limit_bytes=VMEM_LIMIT),
        cost_estimate=pl.CostEstimate(
            flops=8 * 24 * reach_rows * SUBLANES * width, bytes_accessed=5 * 4 * fields * rows * SUBLANES * width, transcendentals=0
        ),
        name="advance",
        **options,
    )(*operands)


def body(ensemble, perturbation, parents, depth):
    per, fields, rows, lon = ensemble.shape
    total_rows = rows * lax.axis_size("lat")
    devices = lax.axis_size("dom")
    me = lax.axis_index("dom").astype(jnp.int32)
    place = lax.axis_index("lat").astype(jnp.int32)[None]
    table, case = plan(parents, me[None], devices, per, ROUNDS + 1)
    tiles = to_tiles(ensemble)
    noise = to_tiles(perturbation)
    count = tiles.shape[2]
    part = count // CHAINS

    def exchange(chains, round_index):
        sends = [select(table, tiles, chain, h * part, part, round_index) for h, chain in enumerate(chains)]
        return [
            chain + [neighbour(up, "dom", 1, True), neighbour(down, "dom", -1, True)]
            for chain, (up, down) in zip(chains, sends)
        ]

    depth_rows = unpack_rows(rows, to_tiles(depth)[None])[0]
    depth_before, depth_after = both_sides(depth_rows)

    chains = [[] for _ in range(CHAINS)]
    for round_index in range(ROUNDS):
        chains = exchange(chains, round_index)
        if round_index == 1:
            chains, depth_before, depth_after = lax.optimization_barrier((chains, depth_before, depth_after))
    depth_strips = (depth_before, depth_rows, depth_after)

    def gather(chains):
        return tuple(collect(table, tiles, noise, chains, rows, k) for k in range(per))

    def all_round(chains):
        own_parents = lax.dynamic_slice_in_dim(parents, me * per, per, 0)

        def turn(k, carry):
            block, found = carry
            block = neighbour(block, "dom", 1, True)
            owner = (me + devices - k - 1) % devices
            found = tuple(
                jnp.where(own_parents[e] // per == owner, block[own_parents[e] % per], found[e]) for e in range(per)
            )
            return block, found

        start = tuple(tiles[own_parents[e] % per] for e in range(per))
        found = lax.fori_loop(0, devices - 1, turn, (tiles, start))[1]
        return tuple(unpack_rows(rows, found[k] + noise[k]) for k in range(per))

    states = lax.switch(
        case[0, 0], [gather, lambda chains: gather(exchange(chains, ROUNDS)), all_round], chains
    )
    for _ in range(STEPS // STEPS_PER_EXCHANGE - 1):
        sides = [both_sides(state) for state in states]
        states = [
            advance((before, state, after), depth_strips, place, total_rows)
            for state, (before, after) in zip(states, sides)
        ]
    result = None
    for member, state in enumerate(states):
        before, after = both_sides(state)
        result = advance((before, state, after), depth_strips, place, total_rows, (member, per, result))
    return from_tiles(result, rows)


def solution(mesh):
    placed = (P("dom", None, "lat", None), P("dom", None, "lat", None), P(), P("lat", None))
    return jax.shard_map(
        body, mesh=mesh, in_specs=placed, out_specs=P("dom", None, "lat", None), check_vma=False
    )
```

```python
import jax
import jax.numpy as jnp
from jax import lax
from jax.experimental import pallas as pl
from jax.experimental.pallas import tpu as pltpu
from jax.sharding import PartitionSpec as P

STEPS = 4
STEPS_PER_EXCHANGE = 2
TIME_STEP = 0.8
LANES = 128
SUBLANES = 8
REACH = 4 * STEPS_PER_EXCHANGE
ROUNDS = 4
CHAINS = 2
UNROLL = 32
VMEM_LIMIT = 16 * 2**20


def to_tiles(strip):
    *lead, rows, lon = strip.shape
    split = strip.reshape(*lead, rows, lon // LANES, LANES)
    return jnp.swapaxes(split, -3, -2).reshape(*lead, lon // LANES * rows, LANES)


def from_tiles(tiles, rows):
    *lead, count, _ = tiles.shape
    split = tiles.reshape(*lead, count // rows, rows, LANES)
    return jnp.swapaxes(split, -3, -2).reshape(*lead, rows, count // rows * LANES)


def neighbour(value, axis, shift, wrap=False):
    devices = lax.axis_size(axis)
    pairs = [(i, (i + shift) % devices) for i in range(devices) if wrap or 0 <= i + shift < devices]
    return lax.ppermute(value, axis, pairs)


def both_sides(value):
    return neighbour(value, "lat", 1), neighbour(value, "lat", -1)


def where_row(row, chunk, rows, chunks):
    return pl.ds(chunk * rows + row, SUBLANES, stride=chunks * rows)


def choose(table_ref, row, identities, candidates):
    wanted = table_ref[row]
    value = candidates[0]
    for identity, candidate in zip(identities[1:], candidates[1:]):
        value = jnp.where(wanted == table_ref[identity], candidate, value)
    return value


def sent_row(per, round_index, direction):
    return 2 * per + 4 * round_index + 2 * direction


def plan_kernel(devices, per, rounds, me_ref, parents_hbm, own_hbm, table_ref, case_ref, own_ref, parents_ref, sems):
    named = pltpu.make_async_copy(parents_hbm, parents_ref, sems.at[0])
    fetched = pltpu.make_async_copy(own_hbm, own_ref, sems.at[1])
    named.start()
    fetched.start()
    count = devices * per
    pairs = 2 * count
    half = devices // 2
    me = me_ref[0]
    slot = lax.broadcasted_iota(jnp.int32, (SUBLANES, LANES), 1)
    item = lax.rem(slot, count)
    direction = slot // count
    origin = item // per
    sibling = item + 1 - 2 * lax.rem(item, 2)
    zero = jnp.zeros((SUBLANES, LANES), jnp.int32)
    reach, opposite, other_opposite, other_up, other_down = zero, zero, zero, zero, zero
    named.wait()
    for entry in range(count):
        parent = parents_ref[entry]
        hops = lax.rem(entry // per - parent // per + devices, devices)
        up = jnp.where(hops < half, hops, 0)
        down = jnp.where(hops > half, devices - hops, 0)
        tie = jnp.where(hops == half, 1, 0)
        mine, other = item == parent, sibling == parent
        reach = jnp.maximum(reach, jnp.where(mine, jnp.where(direction == 0, up, down), 0))
        opposite = jnp.maximum(opposite, jnp.where(mine, tie, 0))
        other_opposite = jnp.maximum(other_opposite, jnp.where(other, tie, 0))
        other_up = jnp.maximum(other_up, jnp.where(other, up, 0))
        other_down = jnp.maximum(other_down, jnp.where(other, down, 0))
    goes_down = jnp.where(
        other_opposite > 0,
        lax.rem(origin + item, 2),
        jnp.where(other_up == other_down, lax.rem(origin, 2), jnp.where(other_up < other_down, 0, 1)),
    )
    reach = jnp.where((opposite > 0) & (goes_down == direction), half, reach)

    down_row = lax.broadcasted_iota(jnp.int32, (pairs, LANES), 0)
    along_row = lax.broadcasted_iota(jnp.int32, (pairs, LANES), 1)

    def facts(index):
        thing = lax.rem(index, count)
        return index // count, thing, thing // per

    sides = [facts(index) for index in (down_row, along_row)]
    far_along = jnp.broadcast_to(reach[:1], (pairs, LANES))
    far_down = jnp.max(jnp.where(down_row == along_row, far_along, 0), axis=1, keepdims=True)
    far = [jnp.broadcast_to(far_down, (pairs, LANES)), far_along]

    def put(row, value):
        table_ref[row] = jnp.broadcast_to(value, (SUBLANES, LANES)).astype(jnp.int32)

    position = [jnp.zeros((pairs, LANES), jnp.int32) for _ in range(2)]
    unmet = []
    for r in range(rounds):
        left, link, key = [], [], []
        for (way, _, start), f, p, index in zip(sides, far, position, (down_row, along_row)):
            step = jnp.where(way == 0, p, devices - p)
            left.append(f - p)
            link.append(lax.rem(start + step, devices) + way * devices)
            key.append(jnp.where(f > p, (f - p) * pairs + pairs - 1 - index, -1))
        same = link[0] == link[1]
        beaten_down = jnp.max(jnp.where(same & (key[1] > key[0]), 1, 0), axis=1, keepdims=True)
        beaten_along = jnp.max(jnp.where(same & (key[0] > key[1]), 1, 0), axis=0, keepdims=True)
        wins = [
            jnp.where((left[0] > 0) & (jnp.broadcast_to(beaten_down, left[0].shape) == 0), 1, 0),
            jnp.where((left[1] > 0) & (jnp.broadcast_to(beaten_along, left[1].shape) == 0), 1, 0),
        ]
        for q, (place, way) in enumerate(((me, 0), (me + devices - 1, 0), (me, 1), (me + 1, 1))):
            here = (wins[1] > 0) & (link[1] == lax.rem(place, devices) + way * devices)
            put(2 * per + 4 * r + q, jnp.max(jnp.where(here, sides[1][1], -1)[:SUBLANES], axis=1, keepdims=True))
        position = [p + w for p, w in zip(position, wins)]
        unmet.append(jnp.max(jnp.where(far[1] > position[1], 1, 0)[:SUBLANES], axis=1, keepdims=True))
    case = jnp.broadcast_to(unmet[-2] + unmet[-1], (SUBLANES, LANES))
    case_ref[...] = case
    for k in range(per):
        put(k, jnp.full((SUBLANES, LANES), me * per + k, jnp.int32))
        entry = jnp.full((SUBLANES, LANES), parents_ref[me * per + k], jnp.int32)
        put(per + k, jnp.where(case == 2, count + k, entry))
        last = sent_row(per, rounds - 1, k) + 1
        table_ref[last] = jnp.where(case == 2, count + k, table_ref[last])
    fetched.wait()


def plan(parents, own, me, devices, per, rounds):
    vmem = pl.BlockSpec(memory_space=pltpu.VMEM)
    hbm = pl.BlockSpec(memory_space=pltpu.HBM)
    return pl.pallas_call(
        lambda *refs: plan_kernel(devices, per, rounds, *refs),
        out_shape=(
            jax.ShapeDtypeStruct((2 * per + 4 * rounds, SUBLANES, LANES), jnp.int32),
            jax.ShapeDtypeStruct((SUBLANES, LANES), jnp.int32),
            jax.ShapeDtypeStruct(own.shape, own.dtype),
        ),
        in_specs=[pl.BlockSpec(memory_space=pltpu.SMEM), hbm, hbm],
        out_specs=(vmem, vmem, vmem),
        scratch_shapes=[pltpu.SMEM(parents.shape, jnp.int32), pltpu.SemaphoreType.DMA((2,))],
        compiler_params=pltpu.CompilerParams(vmem_limit_bytes=VMEM_LIMIT),
        name="plan",
    )(me, parents, own)


def candidates_of(per, own_ref, received, field, base, rows):
    values = [own_ref[k, field, pl.ds(base, rows), :].reshape(-1, SUBLANES, LANES) for k in range(per)]
    return values + [ref[field].reshape(-1, SUBLANES, LANES) for ref in received]


def received_rows(per, direction, received):
    return [sent_row(per, r, direction) + 1 for r in range(received)]


def select_kernel(per, base, direction, table_ref, own_ref, *refs):
    received, out_ref = refs[:-1], refs[-1]
    fields, rows, _ = out_ref.shape
    names = list(range(per)) + received_rows(per, direction, len(received))
    for f in range(fields):
        values = candidates_of(per, own_ref, received, f, base, rows)
        wanted = sent_row(per, len(received), direction)
        out_ref[f] = choose(table_ref, wanted, names, values).reshape(rows, LANES)


def select(table, own, received, base, rows, direction):
    per, fields = own.shape[:2]
    vmem = pl.BlockSpec(memory_space=pltpu.VMEM)
    return pl.pallas_call(
        lambda *refs: select_kernel(per, base, direction, *refs),
        out_shape=jax.ShapeDtypeStruct((fields, rows, LANES), jnp.float32),
        in_specs=[vmem] * (2 + len(received)),
        out_specs=vmem,
        cost_estimate=pl.CostEstimate(flops=0, bytes_accessed=4 * fields * rows * LANES * 4, transcendentals=0),
        compiler_params=pltpu.CompilerParams(vmem_limit_bytes=VMEM_LIMIT),
        name="select",
    )(table, own, *received)


def spread(rows, value_ref, out_ref):
    fields = out_ref.shape[0]
    chunks = out_ref.shape[-1] // LANES

    def one_row(r, carry):
        for f in range(fields):
            for c in range(chunks):
                out_ref[f, r, :, pl.ds(c * LANES, LANES)] = value_ref[f, where_row(r, c, rows, chunks), :]
        return carry

    lax.fori_loop(0, rows, one_row, 0)


def collect_kernel(per, rows, entry, chains, with_depth, table_ref, own_ref, noise_ref, *refs):
    out_ref, value_ref = refs[-2:]
    received = refs[:-2]
    if with_depth:
        depth_ref, received = received[0], received[1:]
        value_ref[value_ref.shape[0] - 1] = depth_ref[...]
    each = len(received) // (2 * chains)
    fields = own_ref.shape[1]
    part = value_ref.shape[1] // chains
    names = list(range(per)) + received_rows(per, 0, each) + received_rows(per, 1, each)
    for f in range(fields):
        for h in range(chains):
            pieces = received[2 * h * each:2 * (h + 1) * each]
            found = choose(table_ref, per + entry, names, candidates_of(per, own_ref, pieces, f, h * part, part))
            where = pl.ds(h * part, part)
            value_ref[f, where, :] = found.reshape(part, LANES) + noise_ref[entry, f, where, :]
    spread(rows, value_ref, out_ref)


def collect(table, own, noise, chains, rows, entry, depth=None):
    per, fields, count, _ = own.shape
    lon = count // rows * LANES
    planes = fields + (depth is not None)
    vmem = pl.BlockSpec(memory_space=pltpu.VMEM)
    operands = [table, own, noise] + ([] if depth is None else [depth])
    operands += [piece for chain in chains for stream in chain for piece in stream]
    return pl.pallas_call(
        lambda *refs: collect_kernel(per, rows, entry, len(chains), depth is not None, *refs),
        out_shape=jax.ShapeDtypeStruct((planes, rows, SUBLANES, lon // SUBLANES), jnp.float32),
        in_specs=[vmem] * len(operands),
        out_specs=vmem,
        scratch_shapes=[pltpu.VMEM((planes, count, LANES), jnp.float32)],
        cost_estimate=pl.CostEstimate(flops=fields * rows * lon, bytes_accessed=12 * fields * rows * lon, transcendentals=0),
        compiler_params=pltpu.CompilerParams(vmem_limit_bytes=VMEM_LIMIT),
        name="collect",
    )(*operands)


def advance_kernel(rows, total_rows, final, place_ref, before, own, after, d_before, d_own, d_after, out_ref, state, first, second, third, depth):
    chunks = state.shape[-1] // LANES
    base_row = place_ref[0] * rows - REACH
    lane = lax.broadcasted_iota(jnp.int32, (SUBLANES, LANES), 1)
    at_start, at_end = lane == 0, lane == LANES - 1

    def lanes(c):
        return pl.ds(c * LANES, LANES)

    def load_row(ref, *index):
        return [ref[(*index, slice(None), lanes(c))] for c in range(chunks)]

    def difference_east(row):
        right = [pltpu.roll(v, 1, 1) for v in row]
        left = [pltpu.roll(v, LANES - 1, 1) for v in row]
        before_ = [pltpu.roll(right[-1], 1, 0)] + right[:-1]
        after_ = left[1:] + [pltpu.roll(left[0], SUBLANES - 1, 0)]
        return [
            jnp.where(at_start, b, r) - jnp.where(at_end, a, l)
            for b, r, a, l in zip(before_, right, after_, left)
        ]

    for block, (strip, d) in enumerate(((before, d_before), (own, d_own), (after, d_after))):
        state[:, block * rows:(block + 1) * rows] = strip[:state.shape[0]]
        depth[block * rows:(block + 1) * rows] = d[state.shape[0]]

    def stage(source, low, high, emit):
        def flux(r):
            return [d * v for d, v in zip(load_row(depth, r), load_row(source, 2, r))]

        def one(r, carry):
            h_before, h_here, f_before, f_here = carry
            h_after, f_after = load_row(source, 0, r + 1), flux(r + 1)
            east, north = load_row(source, 1, r), load_row(source, 2, r)
            row = base_row + r
            turn = 0.8 * ((2 * row + 1).astype(jnp.float32) * (1.0 / total_rows) - 1.0)
            inside = jnp.logical_and(row >= 0, row < total_rows)
            dx_flux = difference_east([a * b for a, b in zip(load_row(depth, r), east)])
            dx_h = difference_east(h_here)
            rate_h = [x + (a - b) for x, a, b in zip(dx_flux, f_before, f_after)]
            rate_u = [x + turn * v for x, v in zip(dx_h, north)]
            rate_v = [(a - b) - turn * u for a, b, u in zip(h_before, h_after, east)]
            emit(r, inside, (rate_h, rate_u, rate_v))
            return h_here, h_after, f_here, f_after

        def several(count):
            def run(r, carry):
                for k in range(count):
                    carry = one(r + k, carry)
                return carry
            return run

        carry = (load_row(source, 0, low - 1), load_row(source, 0, low), flux(low - 1), flux(low))
        trips, rest = divmod(high - low, UNROLL)
        carry = lax.fori_loop(0, trips, lambda i, c: several(UNROLL)(low + UNROLL * i, c), carry)
        several(rest)(high - rest, carry)

    def advance(target, weight):
        def emit(r, inside, rates):
            scale = jnp.where(inside, jnp.float32(weight), jnp.float32(0.0))
            for f, rate in enumerate(rates):
                for c in range(chunks):
                    target[f, r, :, lanes(c)] = state[f, r, :, lanes(c)] + scale * rate[c]
        return emit

    def finish(last):
        def emit(r, inside, rates):
            scale = jnp.where(inside, jnp.float32(TIME_STEP / 12.0), jnp.float32(0.0))
            third_part = jnp.float32(1.0 / 3.0)
            for f, rate in enumerate(rates):
                for c in range(chunks):
                    y, a, b, d = (ref[f, r, :, lanes(c)] for ref in (state, first, second, third))
                    value = ((a - y) + (b + b + d)) * third_part + scale * rate[c]
                    if not last:
                        state[f, r, :, lanes(c)] = value
                    elif final:
                        out_ref[f, where_row(r - REACH, c, rows, chunks), :] = value
                    else:
                        out_ref[f, r - REACH, :, lanes(c)] = value
        return emit

    low, high = 0, 2 * REACH + rows
    for step in range(STEPS_PER_EXCHANGE):
        stage(state, low + 1, high - 1, advance(first, 0.25 * TIME_STEP))
        stage(first, low + 2, high - 2, advance(second, 0.25 * TIME_STEP))
        stage(second, low + 3, high - 3, advance(third, 0.5 * TIME_STEP))
        stage(third, low + 4, high - 4, finish(step == STEPS_PER_EXCHANGE - 1))
        low, high = low + 4, high - 4


def advance(strips, depth_strips, place, total_rows, final=None):
    _, rows, _, width = strips[0].shape
    fields = depth_strips[0].shape[0] - 1
    reach_rows = 2 * REACH + rows
    plane = pltpu.VMEM((fields, reach_rows, SUBLANES, width), jnp.float32)
    vmem = pl.BlockSpec(memory_space=pltpu.VMEM)
    smem = pl.BlockSpec(memory_space=pltpu.SMEM)
    operands = [place, *strips, *depth_strips]
    in_specs = [smem] + [vmem] * 6
    options = {}
    if final is None:
        out_shape, out_specs = (fields, *strips[0].shape[1:]), vmem
    else:
        member, members, partial = final
        count = rows * SUBLANES * width // LANES
        out_shape = (members, fields, count, LANES)
        out_specs = pl.BlockSpec((None, fields, count, LANES), lambda i: (member, 0, 0, 0))
        if partial is not None:
            operands.append(partial)
            in_specs.append(pl.BlockSpec(memory_space=pl.ANY))
            options["input_output_aliases"] = {7: 0}

    def kernel(*refs):
        advance_kernel(rows, total_rows, final is not None, *refs[:7], *refs[-6:])

    return pl.pallas_call(
        kernel,
        grid=(1,),
        out_shape=jax.ShapeDtypeStruct(out_shape, jnp.float32),
        in_specs=in_specs,
        out_specs=out_specs,
        scratch_shapes=[plane] * 4 + [pltpu.VMEM((reach_rows, SUBLANES, width), jnp.float32)],
        compiler_params=pltpu.CompilerParams(vmem_limit_bytes=VMEM_LIMIT),
        cost_estimate=pl.CostEstimate(
            flops=8 * 24 * reach_rows * SUBLANES * width, bytes_accessed=5 * 4 * fields * rows * SUBLANES * width, transcendentals=0
        ),
        name="advance",
        **options,
    )(*operands)


def body(ensemble, perturbation, parents, depth):
    per, fields, rows, lon = ensemble.shape
    total_rows = rows * lax.axis_size("lat")
    devices = lax.axis_size("dom")
    me = lax.axis_index("dom").astype(jnp.int32)
    place = lax.axis_index("lat").astype(jnp.int32)[None]
    table, case, tiles = plan(parents, to_tiles(ensemble), me[None], devices, per, ROUNDS + 1)
    noise = to_tiles(perturbation)
    count = tiles.shape[2]
    part = count // CHAINS

    def fresh(chains):
        return [
            [
                neighbour(select(table, tiles, stream, h * part, part, direction), "dom", 1 - 2 * direction, True)
                for direction, stream in enumerate(chain)
            ]
            for h, chain in enumerate(chains)
        ]

    def extend(chains, pieces):
        return [[stream + [piece] for stream, piece in zip(*pair)] for pair in zip(chains, pieces)]

    chains = [[[], []] for _ in range(CHAINS)]
    for _ in range(ROUNDS):
        chains = extend(chains, fresh(chains))

    def gather(chains):
        depth_tiles = to_tiles(depth)
        return [collect(table, tiles, noise, chains, rows, k, depth_tiles if k == 0 else None) for k in range(per)]

    def all_round(chains):
        own_parents = lax.dynamic_slice_in_dim(parents, me * per, per, 0)

        def turn(k, carry):
            block, found = carry
            block = neighbour(block, "dom", 1, True)
            owner = (me + devices - k - 1) % devices
            found = tuple(
                jnp.where(own_parents[e] // per == owner, block[own_parents[e] % per], found[e]) for e in range(per)
            )
            return block, found

        start = tuple(tiles[own_parents[e] % per] for e in range(per))
        found = lax.fori_loop(0, devices - 1, turn, (tiles, start))[1]
        return [[entry[:, h * part:(h + 1) * part] for entry in found] for h in range(CHAINS)]

    states = lax.switch(
        case[0, 0],
        [gather, lambda chains: gather(extend(chains, fresh(chains))), lambda chains: gather(extend(chains, all_round(chains)))],
        chains,
    )
    depth_strips = None
    for _ in range(STEPS // STEPS_PER_EXCHANGE - 1):
        strips = []
        for state in states:
            before, after = both_sides(state)
            strips.append((before, state, after))
        depth_strips = depth_strips or strips[0]
        states = [advance(strip, depth_strips, place, total_rows) for strip in strips]
    result = None
    for member, state in enumerate(states):
        before, after = both_sides(state)
        result = advance((before, state, after), depth_strips, place, total_rows, (member, per, result))
    return from_tiles(result, rows)


def solution(mesh):
    placed = (P("dom", None, "lat", None), P("dom", None, "lat", None), P(), P("lat", None))
    return jax.shard_map(
        body, mesh=mesh, in_specs=placed, out_specs=P("dom", None, "lat", None), check_vma=False
    )
```

```python
import jax
import jax.numpy as jnp
from jax import lax
from jax.experimental import pallas as pl
from jax.experimental.pallas import tpu as pltpu
from jax.sharding import PartitionSpec as P

STEPS = 4
STEPS_PER_EXCHANGE = 2
TIME_STEP = 0.8
LANES = 128
SUBLANES = 8
REACH = 4 * STEPS_PER_EXCHANGE
ROUNDS = 4
CHAINS = 2
UNROLL = 32
VMEM_LIMIT = 16 * 2**20


def to_tiles(strip):
    *lead, rows, lon = strip.shape
    split = strip.reshape(*lead, rows, lon // LANES, LANES)
    return jnp.swapaxes(split, -3, -2).reshape(*lead, lon // LANES * rows, LANES)


def from_tiles(tiles, rows):
    *lead, count, _ = tiles.shape
    split = tiles.reshape(*lead, count // rows, rows, LANES)
    return jnp.swapaxes(split, -3, -2).reshape(*lead, rows, count // rows * LANES)


def neighbour(value, axis, shift, wrap=False):
    devices = lax.axis_size(axis)
    pairs = [(i, (i + shift) % devices) for i in range(devices) if wrap or 0 <= i + shift < devices]
    return lax.ppermute(value, axis, pairs)


def both_sides(value):
    return neighbour(value, "lat", 1), neighbour(value, "lat", -1)


def where_row(row, chunk, rows, chunks):
    return pl.ds(chunk * rows + row, SUBLANES, stride=chunks * rows)


def choose(table_ref, row, identities, candidates):
    wanted = table_ref[row]
    value = candidates[0]
    for identity, candidate in zip(identities[1:], candidates[1:]):
        value = jnp.where(wanted == table_ref[identity], candidate, value)
    return value


def sent_row(per, round_index, direction):
    return 2 * per + 4 * round_index + 2 * direction


def plan_kernel(devices, per, rounds, me_ref, parents_hbm, own_hbm, table_ref, case_ref, own_ref, parents_ref, sems):
    named = pltpu.make_async_copy(parents_hbm, parents_ref, sems.at[0])
    fetched = pltpu.make_async_copy(own_hbm, own_ref, sems.at[1])
    named.start()
    fetched.start()
    count = devices * per
    pairs = 2 * count
    half = devices // 2
    me = me_ref[0]
    slot = lax.broadcasted_iota(jnp.int32, (SUBLANES, LANES), 1)
    item = lax.rem(slot, count)
    direction = slot // count
    origin = item // per
    sibling = item + 1 - 2 * lax.rem(item, 2)
    zero = jnp.zeros((SUBLANES, LANES), jnp.int32)
    reach, opposite, other_opposite, other_up, other_down = zero, zero, zero, zero, zero
    named.wait()
    for entry in range(count):
        parent = parents_ref[entry]
        hops = lax.rem(entry // per - parent // per + devices, devices)
        up = jnp.where(hops < half, hops, 0)
        down = jnp.where(hops > half, devices - hops, 0)
        tie = jnp.where(hops == half, 1, 0)
        mine, other = item == parent, sibling == parent
        reach = jnp.maximum(reach, jnp.where(mine, jnp.where(direction == 0, up, down), 0))
        opposite = jnp.maximum(opposite, jnp.where(mine, tie, 0))
        other_opposite = jnp.maximum(other_opposite, jnp.where(other, tie, 0))
        other_up = jnp.maximum(other_up, jnp.where(other, up, 0))
        other_down = jnp.maximum(other_down, jnp.where(other, down, 0))
    goes_down = jnp.where(
        other_opposite > 0,
        lax.rem(origin + item, 2),
        jnp.where(other_up == other_down, lax.rem(origin, 2), jnp.where(other_up < other_down, 0, 1)),
    )
    reach = jnp.where((opposite > 0) & (goes_down == direction), half, reach)

    down_row = lax.broadcasted_iota(jnp.int32, (pairs, LANES), 0)
    along_row = lax.broadcasted_iota(jnp.int32, (pairs, LANES), 1)

    def facts(index):
        thing = lax.rem(index, count)
        return index // count, thing, thing // per

    sides = [facts(index) for index in (down_row, along_row)]
    far_along = jnp.broadcast_to(reach[:1], (pairs, LANES))
    far_down = jnp.max(jnp.where(down_row == along_row, far_along, 0), axis=1, keepdims=True)
    far = [jnp.broadcast_to(far_down, (pairs, LANES)), far_along]

    def put(row, value):
        table_ref[row] = jnp.broadcast_to(value, (SUBLANES, LANES)).astype(jnp.int32)

    position = [jnp.zeros((pairs, LANES), jnp.int32) for _ in range(2)]
    unmet = []
    for r in range(rounds):
        left, link, key = [], [], []
        for (way, _, start), f, p, index in zip(sides, far, position, (down_row, along_row)):
            step = jnp.where(way == 0, p, devices - p)
            left.append(f - p)
            link.append(lax.rem(start + step, devices) + way * devices)
            key.append(jnp.where(f > p, (f - p) * pairs + pairs - 1 - index, -1))
        same = link[0] == link[1]
        beaten_down = jnp.max(jnp.where(same & (key[1] > key[0]), 1, 0), axis=1, keepdims=True)
        beaten_along = jnp.max(jnp.where(same & (key[0] > key[1]), 1, 0), axis=0, keepdims=True)
        wins = [
            jnp.where((left[0] > 0) & (jnp.broadcast_to(beaten_down, left[0].shape) == 0), 1, 0),
            jnp.where((left[1] > 0) & (jnp.broadcast_to(beaten_along, left[1].shape) == 0), 1, 0),
        ]
        for q, (place, way) in enumerate(((me, 0), (me + devices - 1, 0), (me, 1), (me + 1, 1))):
            here = (wins[1] > 0) & (link[1] == lax.rem(place, devices) + way * devices)
            put(2 * per + 4 * r + q, jnp.max(jnp.where(here, sides[1][1], -1)[:SUBLANES], axis=1, keepdims=True))
        position = [p + w for p, w in zip(position, wins)]
        unmet.append(jnp.max(jnp.where(far[1] > position[1], 1, 0)[:SUBLANES], axis=1, keepdims=True))
    case = jnp.broadcast_to(unmet[-2] + unmet[-1], (SUBLANES, LANES))
    case_ref[...] = case
    for k in range(per):
        put(k, jnp.full((SUBLANES, LANES), me * per + k, jnp.int32))
        put(per + k, jnp.full((SUBLANES, LANES), parents_ref[me * per + k], jnp.int32))
    fetched.wait()


def plan(parents, own, me, devices, per, rounds):
    vmem = pl.BlockSpec(memory_space=pltpu.VMEM)
    hbm = pl.BlockSpec(memory_space=pltpu.HBM)
    return pl.pallas_call(
        lambda *refs: plan_kernel(devices, per, rounds, *refs),
        out_shape=(
            jax.ShapeDtypeStruct((2 * per + 4 * rounds, SUBLANES, LANES), jnp.int32),
            jax.ShapeDtypeStruct((SUBLANES, LANES), jnp.int32),
            jax.ShapeDtypeStruct(own.shape, own.dtype),
        ),
        in_specs=[pl.BlockSpec(memory_space=pltpu.SMEM), hbm, hbm],
        out_specs=(vmem, vmem, vmem),
        scratch_shapes=[pltpu.SMEM(parents.shape, jnp.int32), pltpu.SemaphoreType.DMA((2,))],
        compiler_params=pltpu.CompilerParams(vmem_limit_bytes=VMEM_LIMIT),
        name="plan",
    )(me, parents, own)


def candidates_of(per, own_ref, received, field, base, rows):
    values = [own_ref[k, field, pl.ds(base, rows), :].reshape(-1, SUBLANES, LANES) for k in range(per)]
    return values + [ref[field].reshape(-1, SUBLANES, LANES) for ref in received]


def received_rows(per, direction, received):
    return [sent_row(per, r, direction) + 1 for r in range(received)]


def select_kernel(per, base, direction, table_ref, own_ref, *refs):
    received, out_ref = refs[:-1], refs[-1]
    fields, rows, _ = out_ref.shape
    names = list(range(per)) + received_rows(per, direction, len(received))
    for f in range(fields):
        values = candidates_of(per, own_ref, received, f, base, rows)
        wanted = sent_row(per, len(received), direction)
        out_ref[f] = choose(table_ref, wanted, names, values).reshape(rows, LANES)


def select(table, own, received, base, rows, direction):
    per, fields = own.shape[:2]
    vmem = pl.BlockSpec(memory_space=pltpu.VMEM)
    return pl.pallas_call(
        lambda *refs: select_kernel(per, base, direction, *refs),
        out_shape=jax.ShapeDtypeStruct((fields, rows, LANES), jnp.float32),
        in_specs=[vmem] * (2 + len(received)),
        out_specs=vmem,
        cost_estimate=pl.CostEstimate(flops=0, bytes_accessed=4 * fields * rows * LANES * 4, transcendentals=0),
        compiler_params=pltpu.CompilerParams(vmem_limit_bytes=VMEM_LIMIT),
        name="select",
    )(table, own, *received)


def spread(rows, value_ref, out_ref):
    fields = out_ref.shape[0]
    chunks = out_ref.shape[-1] // LANES

    def one_row(r, carry):
        for f in range(fields):
            for c in range(chunks):
                out_ref[f, r, :, pl.ds(c * LANES, LANES)] = value_ref[f, where_row(r, c, rows, chunks), :]
        return carry

    lax.fori_loop(0, rows, one_row, 0)


def collect_kernel(per, rows, entry, chains, with_depth, table_ref, own_ref, noise_ref, *refs):
    out_ref, value_ref = refs[-2:]
    received = refs[:-2]
    if with_depth:
        depth_ref, received = received[0], received[1:]
        value_ref[value_ref.shape[0] - 1] = depth_ref[...]
    each = len(received) // (2 * chains)
    fields = own_ref.shape[1]
    part = value_ref.shape[1] // chains
    names = list(range(per)) + received_rows(per, 0, each) + received_rows(per, 1, each)
    for f in range(fields):
        for h in range(chains):
            pieces = received[2 * h * each:2 * (h + 1) * each]
            found = choose(table_ref, per + entry, names, candidates_of(per, own_ref, pieces, f, h * part, part))
            where = pl.ds(h * part, part)
            value_ref[f, where, :] = found.reshape(part, LANES) + noise_ref[entry, f, where, :]
    spread(rows, value_ref, out_ref)


def collect(table, own, noise, chains, rows, entry, depth=None):
    per, fields, count, _ = own.shape
    lon = count // rows * LANES
    planes = fields + (depth is not None)
    vmem = pl.BlockSpec(memory_space=pltpu.VMEM)
    operands = [table, own, noise] + ([] if depth is None else [depth])
    operands += [piece for chain in chains for stream in chain for piece in stream]
    return pl.pallas_call(
        lambda *refs: collect_kernel(per, rows, entry, len(chains), depth is not None, *refs),
        out_shape=jax.ShapeDtypeStruct((planes, rows, SUBLANES, lon // SUBLANES), jnp.float32),
        in_specs=[vmem] * len(operands),
        out_specs=vmem,
        scratch_shapes=[pltpu.VMEM((planes, count, LANES), jnp.float32)],
        cost_estimate=pl.CostEstimate(flops=fields * rows * lon, bytes_accessed=12 * fields * rows * lon, transcendentals=0),
        compiler_params=pltpu.CompilerParams(vmem_limit_bytes=VMEM_LIMIT),
        name="collect",
    )(*operands)


def advance_kernel(rows, total_rows, final, place_ref, before, own, after, d_before, d_own, d_after, out_ref, state, first, second, third, depth):
    chunks = state.shape[-1] // LANES
    base_row = place_ref[0] * rows - REACH
    lane = lax.broadcasted_iota(jnp.int32, (SUBLANES, LANES), 1)
    at_start, at_end = lane == 0, lane == LANES - 1

    def lanes(c):
        return pl.ds(c * LANES, LANES)

    def load_row(ref, *index):
        return [ref[(*index, slice(None), lanes(c))] for c in range(chunks)]

    def difference_east(row):
        right = [pltpu.roll(v, 1, 1) for v in row]
        left = [pltpu.roll(v, LANES - 1, 1) for v in row]
        before_ = [pltpu.roll(right[-1], 1, 0)] + right[:-1]
        after_ = left[1:] + [pltpu.roll(left[0], SUBLANES - 1, 0)]
        return [
            jnp.where(at_start, b, r) - jnp.where(at_end, a, l)
            for b, r, a, l in zip(before_, right, after_, left)
        ]

    for block, (strip, d) in enumerate(((before, d_before), (own, d_own), (after, d_after))):
        state[:, block * rows:(block + 1) * rows] = strip[:state.shape[0]]
        depth[block * rows:(block + 1) * rows] = d[state.shape[0]]

    def stage(source, low, high, emit):
        def flux(r):
            return [d * v for d, v in zip(load_row(depth, r), load_row(source, 2, r))]

        def one(r, carry):
            h_before, h_here, f_before, f_here = carry
            h_after, f_after = load_row(source, 0, r + 1), flux(r + 1)
            east, north = load_row(source, 1, r), load_row(source, 2, r)
            row = base_row + r
            turn = 0.8 * ((2 * row + 1).astype(jnp.float32) * (1.0 / total_rows) - 1.0)
            inside = jnp.logical_and(row >= 0, row < total_rows)
            dx_flux = difference_east([a * b for a, b in zip(load_row(depth, r), east)])
            dx_h = difference_east(h_here)
            rate_h = [x + (a - b) for x, a, b in zip(dx_flux, f_before, f_after)]
            rate_u = [x + turn * v for x, v in zip(dx_h, north)]
            rate_v = [(a - b) - turn * u for a, b, u in zip(h_before, h_after, east)]
            emit(r, inside, (rate_h, rate_u, rate_v))
            return h_here, h_after, f_here, f_after

        def several(count):
            def run(r, carry):
                for k in range(count):
                    carry = one(r + k, carry)
                return carry
            return run

        carry = (load_row(source, 0, low - 1), load_row(source, 0, low), flux(low - 1), flux(low))
        trips, rest = divmod(high - low, UNROLL)
        carry = lax.fori_loop(0, trips, lambda i, c: several(UNROLL)(low + UNROLL * i, c), carry)
        several(rest)(high - rest, carry)

    def advance(target, weight):
        def emit(r, inside, rates):
            scale = jnp.where(inside, jnp.float32(weight), jnp.float32(0.0))
            for f, rate in enumerate(rates):
                for c in range(chunks):
                    target[f, r, :, lanes(c)] = state[f, r, :, lanes(c)] + scale * rate[c]
        return emit

    def finish(last):
        def emit(r, inside, rates):
            scale = jnp.where(inside, jnp.float32(TIME_STEP / 12.0), jnp.float32(0.0))
            third_part = jnp.float32(1.0 / 3.0)
            for f, rate in enumerate(rates):
                for c in range(chunks):
                    y, a, b, d = (ref[f, r, :, lanes(c)] for ref in (state, first, second, third))
                    value = ((a - y) + (b + b + d)) * third_part + scale * rate[c]
                    if not last:
                        state[f, r, :, lanes(c)] = value
                    elif final:
                        out_ref[f, where_row(r - REACH, c, rows, chunks), :] = value
                    else:
                        out_ref[f, r - REACH, :, lanes(c)] = value
        return emit

    low, high = 0, 2 * REACH + rows
    for step in range(STEPS_PER_EXCHANGE):
        stage(state, low + 1, high - 1, advance(first, 0.25 * TIME_STEP))
        stage(first, low + 2, high - 2, advance(second, 0.25 * TIME_STEP))
        stage(second, low + 3, high - 3, advance(third, 0.5 * TIME_STEP))
        stage(third, low + 4, high - 4, finish(step == STEPS_PER_EXCHANGE - 1))
        low, high = low + 4, high - 4


def advance(strips, depth_strips, place, total_rows, final=None):
    _, rows, _, width = strips[0].shape
    fields = depth_strips[0].shape[0] - 1
    reach_rows = 2 * REACH + rows
    plane = pltpu.VMEM((fields, reach_rows, SUBLANES, width), jnp.float32)
    vmem = pl.BlockSpec(memory_space=pltpu.VMEM)
    smem = pl.BlockSpec(memory_space=pltpu.SMEM)
    operands = [place, *strips, *depth_strips]
    in_specs = [smem] + [vmem] * 6
    options = {}
    if final is None:
        out_shape, out_specs = (fields, *strips[0].shape[1:]), vmem
    else:
        member, members, partial = final
        count = rows * SUBLANES * width // LANES
        out_shape = (members, fields, count, LANES)
        out_specs = pl.BlockSpec((None, fields, count, LANES), lambda i: (member, 0, 0, 0))
        if partial is not None:
            operands.append(partial)
            in_specs.append(pl.BlockSpec(memory_space=pl.ANY))
            options["input_output_aliases"] = {7: 0}

    def kernel(*refs):
        advance_kernel(rows, total_rows, final is not None, *refs[:7], *refs[-6:])

    return pl.pallas_call(
        kernel,
        grid=(1,),
        out_shape=jax.ShapeDtypeStruct(out_shape, jnp.float32),
        in_specs=in_specs,
        out_specs=out_specs,
        scratch_shapes=[plane] * 4 + [pltpu.VMEM((reach_rows, SUBLANES, width), jnp.float32)],
        compiler_params=pltpu.CompilerParams(vmem_limit_bytes=VMEM_LIMIT),
        cost_estimate=pl.CostEstimate(
            flops=8 * 24 * reach_rows * SUBLANES * width, bytes_accessed=5 * 4 * fields * rows * SUBLANES * width, transcendentals=0
        ),
        name="advance",
        **options,
    )(*operands)


def body(ensemble, perturbation, parents, depth):
    per, fields, rows, lon = ensemble.shape
    total_rows = rows * lax.axis_size("lat")
    devices = lax.axis_size("dom")
    me = lax.axis_index("dom").astype(jnp.int32)
    place = lax.axis_index("lat").astype(jnp.int32)[None]
    table, case, tiles = plan(parents, to_tiles(ensemble), me[None], devices, per, ROUNDS + 1)
    noise = to_tiles(perturbation)
    count = tiles.shape[2]
    part = count // CHAINS

    def fresh(chains):
        return [
            [
                neighbour(select(table, tiles, stream, h * part, part, direction), "dom", 1 - 2 * direction, True)
                for direction, stream in enumerate(chain)
            ]
            for h, chain in enumerate(chains)
        ]

    def extend(chains, pieces):
        return [[stream + [piece] for stream, piece in zip(*pair)] for pair in zip(chains, pieces)]

    chains = [[[], []] for _ in range(CHAINS)]
    for _ in range(ROUNDS):
        chains = extend(chains, fresh(chains))

    def gather(chains):
        depth_tiles = to_tiles(depth)
        return [collect(table, tiles, noise, chains, rows, k, depth_tiles if k == 0 else None) for k in range(per)]

    def all_round(chains):
        own_parents = lax.dynamic_slice_in_dim(parents, me * per, per, 0)

        def turn(k, carry):
            block, found = carry
            block = neighbour(block, "dom", 1, True)
            owner = (me + devices - k - 1) % devices
            found = tuple(
                jnp.where(own_parents[e] // per == owner, block[own_parents[e] % per], found[e]) for e in range(per)
            )
            return block, found

        start = tuple(tiles[own_parents[e] % per] for e in range(per))
        found = lax.fori_loop(0, devices - 1, turn, (tiles, start))[1]
        states = []
        for k, entry in enumerate(found):
            planes = entry + noise[k]
            if k == 0:
                planes = jnp.concatenate([planes, to_tiles(depth)[None]])
            split = planes.reshape(planes.shape[0], SUBLANES, count // (SUBLANES * rows), rows, LANES)
            states.append(jnp.transpose(split, (0, 3, 1, 2, 4)).reshape(planes.shape[0], rows, SUBLANES, lon // SUBLANES))
        return states

    states = lax.switch(
        case[0, 0],
        [gather, lambda chains: gather(extend(chains, fresh(chains))), all_round],
        chains,
    )
    depth_strips = None
    for _ in range(STEPS // STEPS_PER_EXCHANGE - 1):
        strips = []
        for state in states:
            before, after = both_sides(state)
            strips.append((before, state, after))
        depth_strips = depth_strips or strips[0]
        states = [advance(strip, depth_strips, place, total_rows) for strip in strips]
    result = None
    for member, state in enumerate(states):
        before, after = both_sides(state)
        result = advance((before, state, after), depth_strips, place, total_rows, (member, per, result))
    return from_tiles(result, rows)


def solution(mesh):
    placed = (P("dom", None, "lat", None), P("dom", None, "lat", None), P(), P("lat", None))
    return jax.shard_map(
        body, mesh=mesh, in_specs=placed, out_specs=P("dom", None, "lat", None), check_vma=False
    )
```
